256 devices in a mesh: pipe: 8 (over x, core), seq: 8 (over z), tensor: 4 (over y).
Axes of the slice: x: 4, y: 4, z: 8, core: 2. Of those that a mesh axis runs over, the one named last changes fastest.
Arguments:
- hidden: bfloat16 [8, 1024, 14336], P('pipe', 'seq', 'tensor'), may hold values from -6 to 6
- down_weight: bfloat16 [8, 14336, 8192], P('pipe', 'tensor', 'seq'), may hold values from -0.046875 to 0.046875
- resid: bfloat16 [1024, 8192], P('tensor', 'seq'), may hold values from -42 to 42
- target: bfloat16 [1024, 8192], P('tensor', 'seq'), may hold values from -6 to 6
- gain: float32 [8192], P('seq'), may hold values from 0.1 to 1.9
- query_left: float32 [8, 8192, 32], P('pipe', 'seq'), may hold values from -0.0625 to 0.0625
- query_right: bfloat16 [8, 14336, 32], P('pipe', 'tensor'), may hold values from -0.046875 to 0.046875
- query_core: float32 [8, 1024], P('pipe'), may hold values from -6 to 6
- eigen: float32 [8, 1024], P('pipe'), may hold values from 0.1 to 10
- lengths: int32 [32], replicated, may hold values from 1 to 256, 1024 in all
Outputs:
- scores: float32 [32], P(('seq', 'tensor'))
The draws below stay inside these ranges and needn't reach their ends.
All inputs are finite; a program needn't handle non-finite values.
Results may differ from the reference program's by a relative error of at most 0.0006.
Values may be sent and summed in bfloat16 or wider, within the bound.
No kernel may reach another device: no remote copies, remote signals or barrier semaphores. Data moves between devices by JAX's collectives and lax.ppermute only.
A program may use at most 64 MiB of HBM per device.

```python
import math
import jax
import jax.numpy as jnp
import numpy as np
from jax import lax

D = 8192
FF = 14336
RANK = 32
SEQ_LEN = 1024
LAYERS = 8
DOCS = 32


def draw_resid(key, part):
    first_key, second_key = jax.random.split(jax.random.fold_in(key, 11))
    column = jnp.arange(D, dtype=jnp.float32) / D
    base = jax.random.truncated_normal(first_key, -5.0, 5.0, (SEQ_LEN, D), jnp.float32)
    row_scale = 10.0 ** jax.random.uniform(second_key, (SEQ_LEN, 1), jnp.float32, 0.0, 0.5)
    column_scale = 10.0 ** column
    return (0.15 * base * row_scale * column_scale[None, :]).astype(jnp.bfloat16)


def block_scale(own_key, extent, cuts, low, largest):
    def one(position, parts):
        steps = jax.random.uniform(jax.random.fold_in(jax.random.fold_in(own_key, 6), position), (parts,), jnp.float32, low / len(cuts), largest / len(cuts))
        return jnp.repeat(jnp.exp(steps), extent[position] // parts).reshape((-1,) + (1,) * (len(extent) - position - 1))

    level = one(*cuts[0])
    for cut in cuts[1:]:
        level = level * one(*cut)
    return level


def profile(count, total, bound, skew):
    loads = [(1 << 20) // math.isqrt(rank ** skew) + 1 for rank in range(2, count + 1)]
    spare, given = total - bound - (count - 1), [1] * (count - 1)
    while spare > 0:
        free = [i for i in range(count - 1) if given[i] < bound]
        mass, budget = sum([loads[i] for i in free]), spare
        for i in free:
            more = min(bound - given[i], max(1, budget * loads[i] // mass), spare)
            given[i] = given[i] + more
            spare = spare - more
    return np.array([bound] + given)


def ragged_sizes(rng, count, total, bound, slope):
    if count == 2:
        one = jax.random.randint(rng, (), max(1, total - bound), min(bound, total - 1) + 1)
        return jnp.stack([one, total - one])
    tallies = jnp.asarray(profile(count, total, bound, slope), jnp.int32)
    couples = (count - 1) // 2
    giver, sink = tallies[1:1 + 2 * couples:2], tallies[2:2 + 2 * couples:2]
    room = jnp.minimum(giver - 1, bound - sink)
    shifted = jax.random.randint(jax.random.fold_in(rng, 1), (couples,), 0, 1 << 20) % (room + 1)
    tallies = tallies.at[1:1 + 2 * couples:2].set(giver - shifted).at[2:2 + 2 * couples:2].set(sink + shifted)
    return tallies[jax.random.permutation(jax.random.fold_in(rng, 2), count)]


def centred(rng, extent, deviation, reach, cuts=(), kind=jnp.bfloat16):
    level = block_scale(rng, extent, cuts, -0.22, 0.18) if cuts else 1.0
    result = jax.random.normal(rng, extent, jnp.float32) * deviation * level
    return jnp.minimum(jnp.maximum(result, -reach), reach).astype(kind)


def setup_inputs(seed: int = 0) -> dict:
    key_list = jax.random.split(jax.random.key(seed), 11)
    return {
        "hidden": centred(key_list[0], (LAYERS, SEQ_LEN, FF), 1.0, 6.0, ((0, 8), (1, 8), (2, 4))),
        "down_weight": centred(key_list[1], (LAYERS, FF, D), FF ** -0.5, 0.046875, ((0, 8), (1, 4), (2, 8))),
        "resid": draw_resid(jax.random.fold_in(key_list[10], 71), 0),
        "target": centred(key_list[3], (SEQ_LEN, D), 1.0, 6.0, ((0, 4), (1, 8))),
        "gain": jnp.clip(1.0 + 0.18 * jax.random.normal(key_list[4], (D,), jnp.float32), 0.1, 1.9),
        "query_left": centred(key_list[5], (LAYERS, D, RANK), D ** -0.5, 0.0625, ((0, 8), (1, 8)), jnp.float32),
        "query_right": centred(key_list[6], (LAYERS, FF, RANK), FF ** -0.5, 0.046875, ((0, 8), (1, 4))),
        "query_core": centred(key_list[7], (LAYERS, RANK * RANK), 1.0, 6.0, ((0, 8),), jnp.float32),
        "eigen": jnp.clip(jnp.exp(math.log(10.0) - 4.6051702 * jax.random.uniform(key_list[8], (LAYERS, RANK * RANK), jnp.float32) ** block_scale(key_list[8], (LAYERS, RANK * RANK), ((0, 8),), -0.2, 0.2)), 0.1, 10.0),
        "lengths": ragged_sizes(key_list[9], DOCS, SEQ_LEN, SEQ_LEN // 4, 2).astype(jnp.int32),
    }


def reference(hidden, down_weight, resid, target, gain, query_left, query_right, query_core, eigen, lengths):
    summed = jnp.zeros((SEQ_LEN, D), jnp.float32)
    for layer in range(LAYERS):
        summed = summed + jnp.dot(hidden[layer], down_weight[layer], preferred_element_type=jnp.float32)
    stream = resid.astype(jnp.float32) + summed
    weighted_target = gain[None, :] * target.astype(jnp.float32)
    mean_square = lax.optimization_barrier(jnp.sum(stream * stream, axis=1)) / D
    inner = lax.optimization_barrier(jnp.sum(weighted_target * stream, axis=1))
    root = jnp.sqrt(mean_square + 1e-05)
    grad_stream = weighted_target / root[:, None] - stream * (inner / (D * root * root * root))[:, None]
    ends = jnp.cumsum(lengths).astype(jnp.int32)
    starts = ends - lengths.astype(jnp.int32)
    token = jnp.arange(SEQ_LEN, dtype=jnp.int32)
    member = ((token[None, :] >= starts[:, None]) & (token[None, :] < ends[:, None])).astype(jnp.float32)
    score = jnp.zeros((DOCS,), jnp.float32)
    self_sum = jnp.zeros((DOCS,), jnp.float32)
    for layer in range(LAYERS):
        left_proj = jnp.dot(grad_stream, query_left[layer], precision=lax.Precision.HIGHEST)
        right_proj = jnp.dot(hidden[layer], query_right[layer], preferred_element_type=jnp.float32)
        outer = (left_proj[:, :, None] * right_proj[:, None, :]).reshape(SEQ_LEN, RANK * RANK)
        cores = jnp.dot(member, outer, precision=lax.Precision.HIGHEST)
        scaled = cores / eigen[layer][None, :]
        score = score + lax.optimization_barrier(jnp.sum(query_core[layer][None, :] * scaled, axis=1))
        self_sum = self_sum + lax.optimization_barrier(jnp.sum(cores * scaled, axis=1))
    return score / jnp.sqrt(self_sum + 1e-06)
```

```python
import jax
import jax.numpy as jnp
from jax import lax
from jax.sharding import PartitionSpec as P

D = 8192


def ring_blocks(x, axis):
    count = lax.axis_size(axis)
    half = x.shape[0] // 2
    up = [(i, (i + 1) % count) for i in range(count)]
    down = [(i, (i - 1) % count) for i in range(count)]
    up_low = down_low = x[:half]
    up_high = down_high = x[half:]
    groups = [[x]]
    for _ in range(count // 2 - 1):
        up_low = lax.ppermute(up_low, axis, up)
        down_high = lax.ppermute(down_high, axis, down)
        up_high = lax.ppermute(up_high, axis, up)
        down_low = lax.ppermute(down_low, axis, down)
        groups.append([up_low, up_high, down_low, down_high])
    up_low = lax.ppermute(up_low, axis, up)
    down_high = lax.ppermute(down_high, axis, down)
    groups.append([up_low, down_high])
    return groups


def ring_order(count):
    order = [0]
    for distance in range(1, count // 2):
        order += [-distance, distance]
    return order + [count // 2]


def per_device(
    hidden, down_weight, resid, target, gain, query_left, query_right, query_core, eigen, lengths
):
    layers = lax.axis_size("pipe")
    seqs = lax.axis_size("seq")
    tensors = lax.axis_size("tensor")
    layer = lax.axis_index("pipe")
    seq = lax.axis_index("seq")
    tensor = lax.axis_index("tensor")
    own = hidden[0]
    weight = down_weight[0]
    block_rows, width = own.shape[0], weight.shape[1]
    rank = query_left.shape[2]
    share = block_rows // (tensors * layers)
    strip = share * layers
    f32 = jnp.float32

    right_partial = jnp.dot(own, query_right[0], preferred_element_type=f32)
    right_parts = lax.all_to_all(right_partial.reshape(tensors, strip, rank), "tensor", 0, 0)
    right_proj = jnp.sum(right_parts, axis=0)

    own_left = jnp.transpose(query_left[0])
    left_all = lax.all_to_all(
        jnp.broadcast_to(own_left[None], (layers, rank, width)), "pipe", 0, 0
    ).reshape(layers * rank, width)

    local_blocks = seqs // tensors
    both = jnp.stack([resid, target]).reshape(2, local_blocks, tensors, layers, share, width)
    both = lax.dynamic_index_in_dim(both, layer, axis=3, keepdims=False)
    both = lax.all_to_all(jnp.transpose(both, (2, 0, 1, 3, 4)), "tensor", 0, 0)
    both = jnp.transpose(both, (1, 0, 2, 3, 4)).reshape(2, seqs * share, width)
    resid_rows, target_rows = both[0].astype(f32), both[1].astype(f32)
    weighted = gain[None, :] * target_rows

    groups = ring_blocks(own, "seq")
    products = []
    for pieces in groups:
        rows = pieces[0] if len(pieces) == 1 else jnp.concatenate(pieces, axis=0)
        products.append(jnp.dot(rows, weight, preferred_element_type=f32).astype(jnp.bfloat16))
    reduced = []
    for part in (products[:3], products[3:]):
        stacked = jnp.concatenate(part, axis=0)
        blocks = stacked.shape[0] // block_rows
        sent = jnp.transpose(
            stacked.reshape(blocks, tensors * layers, share, width), (1, 0, 2, 3)
        ).reshape(tensors * layers, blocks * share, width)
        got = lax.all_to_all(sent, ("tensor", "pipe"), 0, 0)
        reduced.append(jnp.sum(got.astype(f32), axis=0).reshape(blocks, share, width))
    summed = jnp.concatenate(reduced, axis=0)
    order = ring_order(seqs)
    by_offset = [order.index(o if o in order else o - seqs) for o in range(seqs)]
    summed = jnp.concatenate([summed[i : i + 1] for i in by_offset], axis=0)
    summed = jnp.roll(summed, seq, axis=0).reshape(seqs * share, width)
    stream = resid_rows + summed

    square_sum = jnp.sum(stream * stream, axis=1)
    inner = jnp.sum(weighted * stream, axis=1)
    projected = lax.dot_general(
        jnp.concatenate([weighted, stream], axis=0),
        left_all,
        (((1,), (1,)), ((), ())),
        precision=lax.Precision.HIGHEST,
        preferred_element_type=f32,
    ).reshape(2, seqs, share, layers, rank)
    projected = jnp.transpose(projected, (3, 1, 2, 0, 4)).reshape(
        layers, seqs, share, 2 * rank
    )
    stats = jnp.stack([square_sum, inner], axis=1).reshape(1, seqs, share, 2)
    packed = jnp.concatenate(
        [projected, jnp.broadcast_to(stats, (layers, seqs, share, 2))], axis=3
    ).reshape(layers * seqs, share, 2 * rank + 2)
    packed = lax.all_to_all(packed, ("pipe", "seq"), 0, 0)
    totals = jnp.sum(packed.reshape(layers, seqs, share, 2 * rank + 2), axis=1)
    totals = totals.reshape(strip, 2 * rank + 2)
    square_sum, inner = totals[:, 2 * rank], totals[:, 2 * rank + 1]
    root = jnp.sqrt(square_sum / D + 1e-05)
    left_proj = (
        totals[:, :rank] / root[:, None]
        - totals[:, rank : 2 * rank] * (inner / (D * root * root * root))[:, None]
    )

    outer = (left_proj[:, :, None] * right_proj[:, None, :]).reshape(strip, rank * rank)
    docs = lengths.shape[0]
    number = jnp.arange(docs, dtype=jnp.int32)
    starts = jnp.sum(jnp.where(number[None, :] < number[:, None], lengths[None, :], 0), axis=1)
    ends = starts + lengths
    token = seq * block_rows + tensor * strip + jnp.arange(strip, dtype=jnp.int32)
    member = ((token[None, :] >= starts[:, None]) & (token[None, :] < ends[:, None])).astype(f32)
    partial_cores = jnp.dot(member, outer, precision=lax.Precision.HIGHEST)
    cores = jnp.sum(lax.all_to_all(partial_cores, ("seq", "tensor"), 0, 0, tiled=True), axis=0)
    scaled = cores / eigen[0]
    terms = jnp.stack([jnp.sum(query_core[0] * scaled), jnp.sum(cores * scaled)])
    terms = jnp.sum(
        lax.all_to_all(jnp.broadcast_to(terms[None], (layers, 2)), "pipe", 0, 0, tiled=True), axis=0
    )
    return (terms[0] / jnp.sqrt(terms[1] + 1e-06)).reshape(1)


def solution(mesh):
    placed = (
        P("pipe", "seq", "tensor"),
        P("pipe", "tensor", "seq"),
        P("tensor", "seq"),
        P("tensor", "seq"),
        P("seq"),
        P("pipe", "seq", None),
        P("pipe", "tensor", None),
        P("pipe", None),
        P("pipe", None),
        P(),
    )
    return jax.shard_map(
        per_device, mesh=mesh, in_specs=placed, out_specs=P(("seq", "tensor")), check_vma=False
    )
```

```python
import functools

import jax
import jax.numpy as jnp
from jax import lax
from jax.experimental import pallas as pl
from jax.experimental.pallas import tpu as pltpu
from jax.sharding import PartitionSpec as P

D = 8192
F32 = jnp.float32
BF16 = jnp.bfloat16
VMEM_BYTES = 16 << 20
PRODUCT_BYTES = 28 << 20
TILES = 4


def exact_dot(a, b, dims):
    return lax.dot_general(
        a, b, (dims, ((), ())), precision=lax.Precision.HIGHEST, preferred_element_type=F32
    )


def product_kernel(count, extras, based, *refs):
    pieces, weight, order, refs = refs[:count], refs[count], refs[count + 1], refs[count + 2 :]
    extra, refs = refs[: 2 * extras], refs[2 * extras :]
    base, refs = (refs[0], refs[1:]) if based else (None, refs)
    out, rows, tiles, total, sems, tile_sems = refs
    depth = tiles.shape[1]

    def fetch(k):
        return pltpu.make_async_copy(
            weight.at[pl.ds(k * depth, depth)], tiles.at[k], tile_sems.at[k]
        )

    copies, first = [], 0
    for k, piece in enumerate(pieces):
        size = piece.shape[0]
        copies.append(pltpu.make_async_copy(piece, rows.at[pl.ds(first, size)], sems.at[k]))
        first += size
    fetch(0).start()
    for copy in copies:
        copy.start()
    for k in range(1, TILES):
        fetch(k).start()
    for copy in copies:
        copy.wait()
    for k in range(TILES):
        fetch(k).wait()
        value = jnp.dot(
            rows[:, k * depth : (k + 1) * depth], tiles[k], preferred_element_type=F32
        )
        if k == 0:
            total[...] = value
        elif k < TILES - 1:
            total[...] += value
    value = (total[...] + value).astype(BF16)
    value = jnp.dot(order[...], value, preferred_element_type=F32)
    for k in range(extras):
        value += jnp.dot(extra[2 * k][...], extra[2 * k + 1][...], preferred_element_type=F32)
    if based:
        value += base[...].astype(F32)
    out[...] = value.astype(BF16)


def product(pieces, weight, order, extra=(), base=None):
    total = sum(p.shape[0] for p in pieces)
    depth, width = weight.shape
    height = order.shape[0]
    anywhere, held = pl.BlockSpec(memory_space=pl.ANY), pl.BlockSpec(memory_space=pltpu.VMEM)
    weight = pltpu.with_memory_space_constraint(weight, pltpu.HBM)
    small = [order, *extra] + ([] if base is None else [base])
    return pl.pallas_call(
        functools.partial(product_kernel, len(pieces), len(extra) // 2, base is not None),
        out_shape=jax.ShapeDtypeStruct((height, width), BF16),
        in_specs=[anywhere] * len(pieces) + [pl.BlockSpec(memory_space=pltpu.HBM)] + [held] * len(small),
        out_specs=held,
        scratch_shapes=[
            pltpu.VMEM((total, depth), BF16),
            pltpu.VMEM((TILES, depth // TILES, width), BF16),
            pltpu.VMEM((total, width), F32),
            pltpu.SemaphoreType.DMA((len(pieces),)),
            pltpu.SemaphoreType.DMA((TILES,)),
        ],
        compiler_params=pltpu.CompilerParams(vmem_limit_bytes=PRODUCT_BYTES),
        cost_estimate=pl.CostEstimate(flops=1 << 20, bytes_accessed=1 << 16, transcendentals=0),
    )(*pieces, weight, *small)


def reduce_rows(got, resid, aim, left, height):
    stream = resid[...] + jnp.sum(got[...].astype(F32), axis=0)
    square = jnp.sum(stream * stream, axis=1, keepdims=True)
    inner = jnp.sum(aim[...] * stream, axis=1, keepdims=True)
    lane = lax.broadcasted_iota(jnp.int32, (height, 128), 1)
    moments = jnp.where(lane == 0, square, jnp.where(lane == 1, inner, 0.0))
    return exact_dot(stream, left[...], ((1,), (1,))), moments


def stats_kernel(got, resid, aim, left, projected, moments):
    projected[...], moments[...] = reduce_rows(got, resid, aim, left, moments.shape[0])


def stats(got, resid, aim, left):
    count = got.shape[1]
    return pl.pallas_call(
        stats_kernel,
        out_shape=(
            jax.ShapeDtypeStruct((count, left.shape[0]), F32),
            jax.ShapeDtypeStruct((count, 128), F32),
        ),
        compiler_params=pltpu.CompilerParams(vmem_limit_bytes=VMEM_BYTES),
    )(got, resid, aim, left)


def pack_kernel(
    layers, share, got, resid, aim, left, first, first_moments, target, order, packed
):
    projected, moments = reduce_rows(got, resid, aim, left, got.shape[1])
    projected = jnp.concatenate([first[...], projected], axis=0)
    moments = jnp.concatenate([first_moments[...], moments], axis=0)
    projected = exact_dot(order[...], projected, ((1,), (0,)))
    moments = exact_dot(order[...], moments, ((1,), (0,)))
    blocks = order.shape[0] // share
    rank = left.shape[0] // layers
    lane = lax.broadcasted_iota(jnp.int32, (blocks, 128), 1)
    sums = jnp.zeros((blocks, 128), F32)
    for i in range(share):
        part = moments[i * blocks : (i + 1) * blocks]
        sums = jnp.where(lane == i, part[:, 0:1], sums)
        sums = jnp.where(lane == share + i, part[:, 1:2], sums)
    for l in range(layers):
        place = pl.ds(l * blocks, blocks)
        for k, source in enumerate((projected, target[...])):
            packed[place, 0, k * 128 : (k + 1) * 128] = jnp.concatenate(
                [
                    source[i * blocks : (i + 1) * blocks, l * rank : (l + 1) * rank]
                    for i in range(share)
                ],
                axis=1,
            )
        packed[place, 0, 256:384] = sums


def pack(layers, share, *operands):
    blocks = operands[-1].shape[0] // share
    return pl.pallas_call(
        functools.partial(pack_kernel, layers, share),
        out_shape=jax.ShapeDtypeStruct((layers * blocks, 1, 384), F32),
        compiler_params=pltpu.CompilerParams(vmem_limit_bytes=VMEM_BYTES),
    )(*operands)


def per_device(
    hidden, down_weight, resid, target, gain, query_left, query_right, query_core, eigen, lengths
):
    layers = lax.axis_size("pipe")
    seqs = lax.axis_size("seq")
    tensors = lax.axis_size("tensor")
    layer = lax.axis_index("pipe")
    seq = lax.axis_index("seq")
    tensor = lax.axis_index("tensor")
    own = hidden[0]
    width = down_weight.shape[2]
    block_rows = own.shape[0]
    rank = query_left.shape[2]
    peers = tensors * layers
    share = block_rows // peers
    strip = share * layers
    local_blocks = seqs // tensors
    half = block_rows // 2
    up = [(i, (i + 1) % seqs) for i in range(seqs)]
    down = [(i, (i - 1) % seqs) for i in range(seqs)]
    tie = lax.optimization_barrier

    def move(pair):
        return lax.ppermute(pair[0], "seq", up), lax.ppermute(pair[1], "seq", down)

    def column(n):
        return jnp.arange(n, dtype=jnp.int32)

    def one_hot(source, count):
        return (source[:, None] == column(count)[None, :]).astype(BF16)

    def layout(slots):
        place = column(peers * slots * share)
        return place // (slots * share), place // share % slots, place % share

    def units(slots, first, count):
        peer, slot, line = layout(slots)
        source = (slot - first) * block_rows + peer * share + line
        inside = (slot >= first) & (slot < first + count)
        return one_hot(jnp.where(inside, source, -1), count * block_rows)

    def exchange(sent):
        return lax.all_to_all(sent.reshape(peers, -1, width), ("tensor", "pipe"), 0, 0)

    low, high = own[:half], own[half:]
    a1 = move((low, high))
    left_own = jnp.broadcast_to(
        jnp.transpose(query_left[0])[None], (layers, rank, width)
    )
    low, high, left_own = tie((low, high, left_own))
    b1 = move((high, low))
    left_all = lax.all_to_all(left_own, "pipe", 0, 0).reshape(layers * rank, width)
    weight = down_weight[0]
    aside = jnp.where(layer // (2 * local_blocks) == 0, resid, target)
    aside = lax.dynamic_slice_in_dim(aside, layer // 2 % local_blocks * block_rows, block_rows, 0)
    right_partial = jnp.dot(own, query_right[0], preferred_element_type=F32)
    right_partial = right_partial.reshape(tensors, strip * rank)
    right_high = lax.reduce_precision(right_partial, 8, 7)
    right_low = (right_partial - right_high).astype(BF16)
    right_rows = jnp.concatenate([right_high.astype(BF16), right_low], axis=0)
    right_rows = jnp.pad(right_rows, ((0, 128 - 2 * tensors), (0, 0)))

    near = 3
    peer, slot, line = layout(near + 1)
    spare = (slot == near) & (line < 2)
    aside_order = one_hot(
        jnp.where(spare, peer * share + layer % 2 * 2 + line, -1), block_rows
    )
    right_order = one_hot(
        jnp.where(spare & (peer % layers == layer), line * tensors + peer // layers, -1), 128
    )
    near_order, middle_order = units(near + 1, 0, 3), units(2, 0, 2)
    pair_order, last_order = units(near + 1, 0, 2), units(near + 1, 2, 1)
    near_order, middle_order, pair_order, last_order, aside_order, right_order, a1, aside = tie(
        (near_order, middle_order, pair_order, last_order, aside_order, right_order, a1, aside)
    )

    a2 = move(a1)
    b1, right_rows = tie((b1, right_rows))
    b2 = move(b1)
    sent = product(
        [own, a1[0], a1[1], b1[1], b1[0]], weight, near_order, (aside_order, aside)
    )
    a2, sent, left_all = tie((a2, sent, left_all))
    got_near = exchange(sent)
    a3 = move(a2)
    b3 = move(b2)
    sent = product([a2[0], a2[1], b2[1], b2[0]], weight, middle_order)
    a3, sent = tie((a3, sent))
    a4 = move(a3)
    b3, sent, got_near = tie((b3, sent, got_near))
    got_middle = exchange(sent)
    sent = product(
        [a3[0], a3[1], b3[1], b3[0]], weight, pair_order, (right_order, right_rows)
    )
    a4, sent, got_middle = tie((a4, sent, got_middle))
    got_far = exchange(product(list(a4), weight, last_order, base=sent))

    turned = jnp.where(tensor < tensors // 2, 1, -1)
    slots = [0, -1, 1, None, -2, 2, -3, 3, seqs // 2, None]
    slot = column(len(slots) * share)
    offset = jnp.zeros_like(slot)
    filled = jnp.ones_like(slot)
    for i, o in enumerate(slots):
        if o is None:
            filled = jnp.where(slot // share == i, 0, filled)
        else:
            offset = jnp.where(slot // share == i, o * turned, offset)
    block = (seq + offset + 2 * seqs) % seqs
    in_order = jnp.where(filled == 1, block * share + slot % share, -1)
    turn = in_order[:, None] == column(seqs * share)[None, :]
    by_line = jnp.where(filled == 1, slot % share * seqs + block, -1)
    order = (column(seqs * share)[:, None] == by_line[None, :]).astype(F32)

    both = got_near[:, near * share : near * share + 2].reshape(
        tensors, 2, local_blocks * share, width
    )
    both = jnp.transpose(both, (1, 0, 2, 3)).reshape(2, seqs * share, width)
    turn = turn.astype(BF16)
    resid_rows = jnp.dot(turn, both[0], preferred_element_type=F32)
    aim_rows = gain[None, :] * jnp.dot(turn, both[1], preferred_element_type=F32)
    right_proj = jnp.sum(got_far[:, near * share : near * share + 2].astype(F32), axis=(0, 1))
    right_proj = right_proj.reshape(strip, rank)
    got_first = jnp.concatenate([got_near, got_middle], axis=1)
    cut = got_first.shape[1]
    first = stats(got_first, resid_rows[:cut], aim_rows[:cut], left_all)
    target_proj = exact_dot(order, exact_dot(aim_rows, left_all, ((1,), (1,))), ((1,), (0,)))
    packed = pack(
        layers,
        share,
        got_far,
        resid_rows[cut:],
        aim_rows[cut:],
        left_all,
        first[0],
        first[1],
        target_proj,
        order,
    )
    packed = lax.all_to_all(packed, ("pipe", "seq"), 0, 0)
    totals = jnp.sum(packed.reshape(layers, seqs, packed.shape[2]), axis=1)
    cut = share * rank
    stream_proj = totals[:, :cut].reshape(strip, rank)
    target_proj = totals[:, cut : 2 * cut].reshape(strip, rank)
    square_sum = totals[:, 2 * cut : 2 * cut + share].reshape(strip, 1)
    inner = totals[:, 2 * cut + share : 2 * cut + 2 * share].reshape(strip, 1)
    root = jnp.sqrt(square_sum / D + 1e-05)
    left_proj = target_proj / root - stream_proj * (inner / (D * root * root * root))

    outer = (left_proj[:, :, None] * right_proj[:, None, :]).reshape(strip, rank * rank)
    number = jnp.arange(lengths.shape[0], dtype=jnp.int32)
    starts = jnp.sum(jnp.where(number[None, :] < number[:, None], lengths[None, :], 0), axis=1)
    ends = starts + lengths
    token = seq * block_rows + tensor * strip + jnp.arange(strip, dtype=jnp.int32)
    member = ((token[None, :] >= starts[:, None]) & (token[None, :] < ends[:, None])).astype(F32)
    partial_cores = jnp.dot(member, outer, precision=lax.Precision.HIGHEST)
    cores = jnp.sum(lax.all_to_all(partial_cores, ("seq", "tensor"), 0, 0, tiled=True), axis=0)
    scaled = cores / eigen[0]
    terms = jnp.stack([jnp.sum(query_core[0] * scaled), jnp.sum(cores * scaled)])
    terms = jnp.sum(
        lax.all_to_all(jnp.broadcast_to(terms[None], (layers, 2)), "pipe", 0, 0, tiled=True), axis=0
    )
    return (terms[0] / jnp.sqrt(terms[1] + 1e-06)).reshape(1)


def solution(mesh):
    placed = (
        P("pipe", "seq", "tensor"),
        P("pipe", "tensor", "seq"),
        P("tensor", "seq"),
        P("tensor", "seq"),
        P("seq"),
        P("pipe", "seq", None),
        P("pipe", "tensor", None),
        P("pipe", None),
        P("pipe", None),
        P(),
    )
    return jax.shard_map(
        per_device, mesh=mesh, in_specs=placed, out_specs=P(("seq", "tensor")), check_vma=False
    )
```

```python
import functools

import jax
import jax.numpy as jnp
from jax import lax
from jax.experimental import pallas as pl
from jax.experimental.pallas import tpu as pltpu
from jax.sharding import PartitionSpec as P

D = 8192
F32 = jnp.float32
BF16 = jnp.bfloat16
VMEM_BYTES = 16 << 20
PRODUCT_BYTES = 28 << 20
TILES = 4
CHUNK = 256
FLOPS_PER_MICRO = 1_150_000_000


def exact_dot(a, b, dims):
    return lax.dot_general(
        a, b, (dims, ((), ())), precision=lax.Precision.HIGHEST, preferred_element_type=F32
    )


def product_kernel(count, extras, based, *refs):
    pieces, weight, order, refs = refs[:count], refs[count], refs[count + 1], refs[count + 2 :]
    extra, refs = refs[: 2 * extras], refs[2 * extras :]
    base, refs = (refs[0], refs[1:]) if based else (None, refs)
    out, rows, tiles, sums, result, start, sems, tile_sems, out_sems, base_sem = refs
    depth = tiles.shape[1]

    def fetch(k):
        return pltpu.make_async_copy(
            weight.at[pl.ds(k * depth, depth)], tiles.at[k], tile_sems.at[k]
        )

    copies, first = [], 0
    for k, piece in enumerate(pieces):
        size = piece.shape[0]
        copies.append(pltpu.make_async_copy(piece, rows.at[pl.ds(first, size)], sems.at[k]))
        first += size
    fetch(0).start()
    for copy in copies:
        copy.start()
    for k in range(1, TILES):
        fetch(k).start()
    if based:
        first_rows = pltpu.make_async_copy(base, start, base_sem)
        first_rows.start()
    for copy in copies:
        copy.wait()
    for k in range(TILES):
        fetch(k).wait()
        value = jnp.dot(
            rows[:, k * depth : (k + 1) * depth], tiles[k], preferred_element_type=F32
        )
        if k == 0:
            sums[...] = value
        elif k < TILES - 1:
            sums[...] += value
    value = (sums[...] + value).astype(BF16)
    if based:
        first_rows.wait()
    stores = []
    for k in range(out.shape[0] // CHUNK):
        cut = pl.ds(k * CHUNK, CHUNK)
        part = jnp.dot(order[cut, :], value, preferred_element_type=F32)
        for m in range(extras):
            part += jnp.dot(
                extra[2 * m][cut, :], extra[2 * m + 1][...], preferred_element_type=F32
            )
        if based:
            part += start[cut, :].astype(F32)
        result[cut, :] = part.astype(BF16)
        stores.append(pltpu.make_async_copy(result.at[cut], out.at[cut], out_sems.at[k]))
        stores[-1].start()
    for store in stores:
        store.wait()


def product(micros, pieces, weight, order, extra=(), base=None):
    total = sum(p.shape[0] for p in pieces)
    depth, width = weight.shape
    height = order.shape[0]
    based = base is not None
    anywhere, held = pl.BlockSpec(memory_space=pltpu.HBM), pl.BlockSpec(memory_space=pltpu.VMEM)
    far = pltpu.with_memory_space_constraint
    weight = pltpu.with_memory_space_constraint(weight, pltpu.HBM)
    pieces = [far(p, pltpu.HBM) for p in pieces]
    bases = [far(base, pltpu.HBM)] if based else []
    small = [order, *extra]
    return pl.pallas_call(
        functools.partial(product_kernel, len(pieces), len(extra) // 2, based),
        out_shape=pltpu.HBM((height, width), BF16),
        in_specs=[anywhere] * len(pieces) + [pl.BlockSpec(memory_space=pltpu.HBM)] + [held] * len(small) + [anywhere] * len(bases),
        out_specs=anywhere,
        scratch_shapes=[
            pltpu.VMEM((total, depth), BF16),
            pltpu.VMEM((TILES, depth // TILES, width), BF16),
            pltpu.VMEM((total, width), F32),
            pltpu.VMEM((height, width), BF16),
            pltpu.VMEM((height if based else CHUNK, width), BF16),
            pltpu.SemaphoreType.DMA((len(pieces),)),
            pltpu.SemaphoreType.DMA((TILES,)),
            pltpu.SemaphoreType.DMA((height // CHUNK,)),
            pltpu.SemaphoreType.DMA,
        ],
        compiler_params=pltpu.CompilerParams(vmem_limit_bytes=PRODUCT_BYTES),
        cost_estimate=pl.CostEstimate(
            flops=micros * FLOPS_PER_MICRO, bytes_accessed=1 << 16, transcendentals=0
        ),
    )(*pieces, weight, *small, *bases)


def reduce_rows(got, resid, aim, left, height):
    stream = resid[...] + jnp.sum(got[...].astype(F32), axis=0)
    square = jnp.sum(stream * stream, axis=1, keepdims=True)
    inner = jnp.sum(aim[...] * stream, axis=1, keepdims=True)
    lane = lax.broadcasted_iota(jnp.int32, (height, 128), 1)
    moments = jnp.where(lane == 0, square, jnp.where(lane == 1, inner, 0.0))
    return exact_dot(stream, left[...], ((1,), (1,))), moments


def stats_kernel(got, resid, aim, left, projected, moments):
    projected[...], moments[...] = reduce_rows(got, resid, aim, left, moments.shape[0])


def stats(got, resid, aim, left):
    count = got.shape[1]
    return pl.pallas_call(
        stats_kernel,
        out_shape=(
            jax.ShapeDtypeStruct((count, left.shape[0]), F32),
            jax.ShapeDtypeStruct((count, 128), F32),
        ),
        compiler_params=pltpu.CompilerParams(vmem_limit_bytes=VMEM_BYTES),
    )(got, resid, aim, left)


def pack_kernel(
    layers, share, got, resid, aim, left, first, first_moments, target, order, packed
):
    projected, moments = reduce_rows(got, resid, aim, left, got.shape[1])
    projected = jnp.concatenate([first[...], projected], axis=0)
    moments = jnp.concatenate([first_moments[...], moments], axis=0)
    projected = exact_dot(order[...], projected, ((1,), (0,)))
    moments = exact_dot(order[...], moments, ((1,), (0,)))
    blocks = order.shape[0] // share
    rank = left.shape[0] // layers
    lane = lax.broadcasted_iota(jnp.int32, (blocks, 128), 1)
    sums = jnp.zeros((blocks, 128), F32)
    for i in range(share):
        part = moments[i * blocks : (i + 1) * blocks]
        sums = jnp.where(lane == i, part[:, 0:1], sums)
        sums = jnp.where(lane == share + i, part[:, 1:2], sums)
    for l in range(layers):
        place = pl.ds(l * blocks, blocks)
        for k, source in enumerate((projected, target[...])):
            packed[place, 0, k * 128 : (k + 1) * 128] = jnp.concatenate(
                [
                    source[i * blocks : (i + 1) * blocks, l * rank : (l + 1) * rank]
                    for i in range(share)
                ],
                axis=1,
            )
        packed[place, 0, 256:384] = sums


def pack(layers, share, *operands):
    blocks = operands[-1].shape[0] // share
    return pl.pallas_call(
        functools.partial(pack_kernel, layers, share),
        out_shape=jax.ShapeDtypeStruct((layers * blocks, 1, 384), F32),
        compiler_params=pltpu.CompilerParams(vmem_limit_bytes=VMEM_BYTES),
    )(*operands)


def per_device(
    hidden, down_weight, resid, target, gain, query_left, query_right, query_core, eigen, lengths
):
    layers = lax.axis_size("pipe")
    seqs = lax.axis_size("seq")
    tensors = lax.axis_size("tensor")
    layer = lax.axis_index("pipe")
    seq = lax.axis_index("seq")
    tensor = lax.axis_index("tensor")
    own = hidden[0]
    width = down_weight.shape[2]
    block_rows = own.shape[0]
    rank = query_left.shape[2]
    peers = tensors * layers
    share = block_rows // peers
    strip = share * layers
    local_blocks = seqs // tensors
    half = block_rows // 2
    up = [(i, (i + 1) % seqs) for i in range(seqs)]
    down = [(i, (i - 1) % seqs) for i in range(seqs)]
    tie = lax.optimization_barrier

    def move(pair):
        return lax.ppermute(pair[0], "seq", up), lax.ppermute(pair[1], "seq", down)

    def column(n):
        return jnp.arange(n, dtype=jnp.int32)

    def one_hot(source, count):
        return (source[:, None] == column(count)[None, :]).astype(BF16)

    def layout(slots):
        place = column(peers * slots * share)
        return place // (slots * share), place // share % slots, place % share

    def units(slots, first, count):
        peer, slot, line = layout(slots)
        source = (slot - first) * block_rows + peer * share + line
        inside = (slot >= first) & (slot < first + count)
        return one_hot(jnp.where(inside, source, -1), count * block_rows)

    def exchange(sent):
        return lax.all_to_all(sent.reshape(peers, -1, width), ("tensor", "pipe"), 0, 0)

    low, high = own[:half], own[half:]
    a1 = move((low, high))
    left_own = jnp.broadcast_to(
        jnp.transpose(query_left[0])[None], (layers, rank, width)
    )
    low, high, left_own = tie((low, high, left_own))
    b1 = move((high, low))
    left_all = lax.all_to_all(left_own, "pipe", 0, 0).reshape(layers * rank, width)
    weight = down_weight[0]
    aside = jnp.where(layer // (2 * local_blocks) == 0, resid, target)
    aside = lax.dynamic_slice_in_dim(aside, layer // 2 % local_blocks * block_rows, block_rows, 0)
    right_partial = jnp.dot(own, query_right[0], preferred_element_type=F32)
    right_partial = right_partial.reshape(tensors, strip * rank)
    right_high = lax.reduce_precision(right_partial, 8, 7)
    right_low = (right_partial - right_high).astype(BF16)
    right_rows = jnp.concatenate([right_high.astype(BF16), right_low], axis=0)
    right_rows = jnp.pad(right_rows, ((0, 128 - 2 * tensors), (0, 0)))

    near, far = 6, 4
    peer, slot, line = layout(near)
    spare = slot == near - 1
    aside_order = one_hot(
        jnp.where(spare & (line < 2), peer * share + layer % 2 * 2 + line, -1), block_rows
    )
    right_order = one_hot(
        jnp.where(
            spare & (line >= 2) & (peer % layers == layer),
            (line - 2) * tensors + peer // layers,
            -1,
        ),
        128,
    )
    orders = units(near, 0, 3), units(near, 3, 2), units(far, 0, 2), units(far, 2, 1)
    orders, aside_order, right_order, a1, aside = tie((orders, aside_order, right_order, a1, aside))

    a2 = move(a1)
    b1, right_rows = tie((b1, right_rows))
    b2 = move(b1)
    sent = product(1,
        [own, a1[0], a1[1], b1[1], b1[0]], weight, orders[0], (aside_order, aside)
    )
    a2, sent, left_all = tie((a2, sent, left_all))
    a3 = move(a2)
    b3 = move(b2)
    sent = product(6,
        [a2[0], a2[1], b2[1], b2[0]], weight, orders[1], (right_order, right_rows), base=sent
    )
    got_near = exchange(sent)
    a3, sent = tie((a3, sent))
    a4 = move(a3)
    sent = product(6, [a3[0], a3[1], b3[1], b3[0]], weight, orders[2])
    a4, sent = tie((a4, sent))
    sent = product(6, list(a4), weight, orders[3], base=sent)
    sent, got_near = tie((sent, got_near))
    got_far = exchange(sent)

    turned = jnp.where(tensor < tensors // 2, 1, -1)
    slots = [0, -1, 1, -2, 2, None, -3, 3, seqs // 2, None]
    slot = column(len(slots) * share)
    offset = jnp.zeros_like(slot)
    filled = jnp.ones_like(slot)
    for i, o in enumerate(slots):
        if o is None:
            filled = jnp.where(slot // share == i, 0, filled)
        else:
            offset = jnp.where(slot // share == i, o * turned, offset)
    block = (seq + offset + 2 * seqs) % seqs
    in_order = jnp.where(filled == 1, block * share + slot % share, -1)
    turn = in_order[:, None] == column(seqs * share)[None, :]
    by_line = jnp.where(filled == 1, slot % share * seqs + block, -1)
    order = (column(seqs * share)[:, None] == by_line[None, :]).astype(F32)

    cut = near * share
    both = got_near[:, cut - share : cut - share + 2].reshape(
        tensors, 2, local_blocks * share, width
    )
    both = jnp.transpose(both, (1, 0, 2, 3)).reshape(2, seqs * share, width)
    turn = turn.astype(BF16)
    resid_rows = jnp.dot(turn, both[0], preferred_element_type=F32)
    aim_rows = gain[None, :] * jnp.dot(turn, both[1], preferred_element_type=F32)
    right_proj = jnp.sum(got_near[:, cut - share + 2 :].astype(F32), axis=(0, 1))
    right_proj = right_proj.reshape(strip, rank)
    first = stats(got_near, resid_rows[:cut], aim_rows[:cut], left_all)
    target_proj = exact_dot(order, exact_dot(aim_rows, left_all, ((1,), (1,))), ((1,), (0,)))
    packed = pack(
        layers,
        share,
        got_far,
        resid_rows[cut:],
        aim_rows[cut:],
        left_all,
        first[0],
        first[1],
        target_proj,
        order,
    )
    packed = lax.all_to_all(packed, ("pipe", "seq"), 0, 0)
    totals = jnp.sum(packed.reshape(layers, seqs, packed.shape[2]), axis=1)
    cut = share * rank
    stream_proj = totals[:, :cut].reshape(strip, rank)
    target_proj = totals[:, cut : 2 * cut].reshape(strip, rank)
    square_sum = totals[:, 2 * cut : 2 * cut + share].reshape(strip, 1)
    inner = totals[:, 2 * cut + share : 2 * cut + 2 * share].reshape(strip, 1)
    root = jnp.sqrt(square_sum / D + 1e-05)
    left_proj = target_proj / root - stream_proj * (inner / (D * root * root * root))

    outer = (left_proj[:, :, None] * right_proj[:, None, :]).reshape(strip, rank * rank)
    number = jnp.arange(lengths.shape[0], dtype=jnp.int32)
    starts = jnp.sum(jnp.where(number[None, :] < number[:, None], lengths[None, :], 0), axis=1)
    ends = starts + lengths
    token = seq * block_rows + tensor * strip + jnp.arange(strip, dtype=jnp.int32)
    member = ((token[None, :] >= starts[:, None]) & (token[None, :] < ends[:, None])).astype(F32)
    partial_cores = jnp.dot(member, outer, precision=lax.Precision.HIGHEST)
    cores = jnp.sum(lax.all_to_all(partial_cores, ("seq", "tensor"), 0, 0, tiled=True), axis=0)
    scaled = cores / eigen[0]
    terms = jnp.stack([jnp.sum(query_core[0] * scaled), jnp.sum(cores * scaled)])
    terms = jnp.sum(
        lax.all_to_all(jnp.broadcast_to(terms[None], (layers, 2)), "pipe", 0, 0, tiled=True), axis=0
    )
    return (terms[0] / jnp.sqrt(terms[1] + 1e-06)).reshape(1)


def solution(mesh):
    placed = (
        P("pipe", "seq", "tensor"),
        P("pipe", "tensor", "seq"),
        P("tensor", "seq"),
        P("tensor", "seq"),
        P("seq"),
        P("pipe", "seq", None),
        P("pipe", "tensor", None),
        P("pipe", None),
        P("pipe", None),
        P(),
    )
    return jax.shard_map(
        per_device, mesh=mesh, in_specs=placed, out_specs=P(("seq", "tensor")), check_vma=False
    )
```

```python
import functools

import jax
import jax.numpy as jnp
from jax import lax
from jax.experimental import pallas as pl
from jax.experimental.pallas import tpu as pltpu
from jax.sharding import PartitionSpec as P

D = 8192
F32 = jnp.float32
BF16 = jnp.bfloat16
VMEM_BYTES = 16 << 20
PRODUCT_BYTES = 28 << 20
TILES = 4
CHUNK = 256
FLOPS_PER_MICRO = 1_150_000_000


def exact_dot(a, b, dims):
    return lax.dot_general(
        a, b, (dims, ((), ())), precision=lax.Precision.HIGHEST, preferred_element_type=F32
    )


def product_kernel(count, extras, based, *refs):
    pieces, weight, order, refs = refs[:count], refs[count], refs[count + 1], refs[count + 2 :]
    extra, refs = refs[: 2 * extras], refs[2 * extras :]
    base, refs = (refs[0], refs[1:]) if based else (None, refs)
    out, rows, tiles, sums, result, start, sems, tile_sems, out_sems, base_sem = refs
    depth = tiles.shape[1]

    def fetch(k):
        return pltpu.make_async_copy(
            weight.at[pl.ds(k * depth, depth)], tiles.at[k], tile_sems.at[k]
        )

    copies, first = [], 0
    for k, piece in enumerate(pieces):
        size = piece.shape[0]
        copies.append(pltpu.make_async_copy(piece, rows.at[pl.ds(first, size)], sems.at[k]))
        first += size
    fetch(0).start()
    for copy in copies:
        copy.start()
    for k in range(1, TILES):
        fetch(k).start()
    if based:
        first_rows = pltpu.make_async_copy(base, start, base_sem)
        first_rows.start()
    for copy in copies:
        copy.wait()
    for k in range(TILES):
        fetch(k).wait()
        value = jnp.dot(
            rows[:, k * depth : (k + 1) * depth], tiles[k], preferred_element_type=F32
        )
        if k == 0:
            sums[...] = value
        elif k < TILES - 1:
            sums[...] += value
    value = (sums[...] + value).astype(BF16)
    if based:
        first_rows.wait()
    stores = []
    for k in range(out.shape[0] // CHUNK):
        cut = pl.ds(k * CHUNK, CHUNK)
        part = jnp.dot(order[cut, :], value, preferred_element_type=F32)
        for m in range(extras):
            part += jnp.dot(
                extra[2 * m][cut, :], extra[2 * m + 1][...], preferred_element_type=F32
            )
        if based:
            part += start[cut, :].astype(F32)
        result[cut, :] = part.astype(BF16)
        stores.append(pltpu.make_async_copy(result.at[cut], out.at[cut], out_sems.at[k]))
        stores[-1].start()
    for store in stores:
        store.wait()


def product(micros, pieces, weight, order, extra=(), base=None):
    total = sum(p.shape[0] for p in pieces)
    depth, width = weight.shape
    height = order.shape[0]
    based = base is not None
    anywhere, held = pl.BlockSpec(memory_space=pltpu.HBM), pl.BlockSpec(memory_space=pltpu.VMEM)
    far = pltpu.with_memory_space_constraint
    weight = pltpu.with_memory_space_constraint(weight, pltpu.HBM)
    bases = [far(base, pltpu.HBM)] if based else []
    small = [order, *extra]
    return pl.pallas_call(
        functools.partial(product_kernel, len(pieces), len(extra) // 2, based),
        out_shape=pltpu.HBM((height, width), BF16),
        in_specs=[pl.BlockSpec(memory_space=pl.ANY)] * len(pieces) + [pl.BlockSpec(memory_space=pltpu.HBM)] + [held] * len(small) + [anywhere] * len(bases),
        out_specs=anywhere,
        scratch_shapes=[
            pltpu.VMEM((total, depth), BF16),
            pltpu.VMEM((TILES, depth // TILES, width), BF16),
            pltpu.VMEM((total, width), F32),
            pltpu.VMEM((height, width), BF16),
            pltpu.VMEM((height if based else CHUNK, width), BF16),
            pltpu.SemaphoreType.DMA((len(pieces),)),
            pltpu.SemaphoreType.DMA((TILES,)),
            pltpu.SemaphoreType.DMA((height // CHUNK,)),
            pltpu.SemaphoreType.DMA,
        ],
        compiler_params=pltpu.CompilerParams(vmem_limit_bytes=PRODUCT_BYTES),
        cost_estimate=pl.CostEstimate(
            flops=micros * FLOPS_PER_MICRO, bytes_accessed=1 << 16, transcendentals=0
        ),
    )(*pieces, weight, *small, *bases)


def reduce_rows(got, resid, aim, left, height):
    stream = resid[...] + jnp.sum(got[...].astype(F32), axis=0)
    square = jnp.sum(stream * stream, axis=1, keepdims=True)
    inner = jnp.sum(aim[...] * stream, axis=1, keepdims=True)
    lane = lax.broadcasted_iota(jnp.int32, (height, 128), 1)
    moments = jnp.where(lane == 0, square, jnp.where(lane == 1, inner, 0.0))
    return exact_dot(stream, left[...], ((1,), (1,))), moments


def stats_kernel(got, resid, aim, left, projected, moments):
    projected[...], moments[...] = reduce_rows(got, resid, aim, left, moments.shape[0])


def stats(got, resid, aim, left):
    count = got.shape[1]
    return pl.pallas_call(
        stats_kernel,
        out_shape=(
            jax.ShapeDtypeStruct((count, left.shape[0]), F32),
            jax.ShapeDtypeStruct((count, 128), F32),
        ),
        compiler_params=pltpu.CompilerParams(vmem_limit_bytes=VMEM_BYTES),
    )(got, resid, aim, left)


def pack_kernel(
    layers, share, got, resid, aim, left, first, first_moments, target, order, packed
):
    projected, moments = reduce_rows(got, resid, aim, left, got.shape[1])
    projected = jnp.concatenate([first[...], projected], axis=0)
    moments = jnp.concatenate([first_moments[...], moments], axis=0)
    projected = exact_dot(order[...], projected, ((1,), (0,)))
    moments = exact_dot(order[...], moments, ((1,), (0,)))
    blocks = order.shape[0] // share
    rank = left.shape[0] // layers
    lane = lax.broadcasted_iota(jnp.int32, (blocks, 128), 1)
    sums = jnp.zeros((blocks, 128), F32)
    for i in range(share):
        part = moments[i * blocks : (i + 1) * blocks]
        sums = jnp.where(lane == i, part[:, 0:1], sums)
        sums = jnp.where(lane == share + i, part[:, 1:2], sums)
    for l in range(layers):
        place = pl.ds(l * blocks, blocks)
        for k, source in enumerate((projected, target[...])):
            packed[place, 0, k * 128 : (k + 1) * 128] = jnp.concatenate(
                [
                    source[i * blocks : (i + 1) * blocks, l * rank : (l + 1) * rank]
                    for i in range(share)
                ],
                axis=1,
            )
        packed[place, 0, 256:384] = sums


def pack(layers, share, *operands):
    blocks = operands[-1].shape[0] // share
    return pl.pallas_call(
        functools.partial(pack_kernel, layers, share),
        out_shape=jax.ShapeDtypeStruct((layers * blocks, 1, 384), F32),
        compiler_params=pltpu.CompilerParams(vmem_limit_bytes=VMEM_BYTES),
    )(*operands)


def per_device(
    hidden, down_weight, resid, target, gain, query_left, query_right, query_core, eigen, lengths
):
    layers = lax.axis_size("pipe")
    seqs = lax.axis_size("seq")
    tensors = lax.axis_size("tensor")
    layer = lax.axis_index("pipe")
    seq = lax.axis_index("seq")
    tensor = lax.axis_index("tensor")
    own = hidden[0]
    width = down_weight.shape[2]
    block_rows = own.shape[0]
    rank = query_left.shape[2]
    peers = tensors * layers
    share = block_rows // peers
    strip = share * layers
    local_blocks = seqs // tensors
    half = block_rows // 2
    up = [(i, (i + 1) % seqs) for i in range(seqs)]
    down = [(i, (i - 1) % seqs) for i in range(seqs)]
    tie = lax.optimization_barrier

    def move(pair):
        return lax.ppermute(pair[0], "seq", up), lax.ppermute(pair[1], "seq", down)

    def column(n):
        return jnp.arange(n, dtype=jnp.int32)

    def one_hot(source, count):
        return (source[:, None] == column(count)[None, :]).astype(BF16)

    def layout(slots):
        place = column(peers * slots * share)
        return place // (slots * share), place // share % slots, place % share

    def units(slots, first, count):
        peer, slot, line = layout(slots)
        source = (slot - first) * block_rows + peer * share + line
        inside = (slot >= first) & (slot < first + count)
        return one_hot(jnp.where(inside, source, -1), count * block_rows)

    def exchange(sent):
        return lax.all_to_all(sent.reshape(peers, -1, width), ("tensor", "pipe"), 0, 0)

    low, high = own[:half], own[half:]
    a1 = move((low, high))
    left_own = jnp.broadcast_to(
        jnp.transpose(query_left[0])[None], (layers, rank, width)
    )
    low, high, left_own = tie((low, high, left_own))
    b1 = move((high, low))
    left_all = lax.all_to_all(left_own, "pipe", 0, 0).reshape(layers * rank, width)
    weight = down_weight[0]
    aside = jnp.where(layer // (2 * local_blocks) == 0, resid, target)
    aside = lax.dynamic_slice_in_dim(aside, layer // 2 % local_blocks * block_rows, block_rows, 0)
    right_partial = jnp.dot(own, query_right[0], preferred_element_type=F32)
    right_partial = right_partial.reshape(tensors, strip * rank)
    right_high = lax.reduce_precision(right_partial, 8, 7)
    right_low = (right_partial - right_high).astype(BF16)
    right_rows = jnp.concatenate([right_high.astype(BF16), right_low], axis=0)
    right_rows = jnp.pad(right_rows, ((0, 128 - 2 * tensors), (0, 0)))

    near, far = 6, 4
    peer, slot, line = layout(near)
    spare = slot == near - 1
    aside_order = one_hot(
        jnp.where(spare & (line < 2), peer * share + layer % 2 * 2 + line, -1), block_rows
    )
    right_order = one_hot(
        jnp.where(
            spare & (line >= 2) & (peer % layers == layer),
            (line - 2) * tensors + peer // layers,
            -1,
        ),
        128,
    )
    orders = units(near, 0, 3), units(near, 3, 1), units(far, 0, 3), units(far, 3, 1)
    orders, aside_order, right_order, a1, aside = tie((orders, aside_order, right_order, a1, aside))

    a2 = move(a1)
    b1, right_rows = tie((b1, right_rows))
    b2 = move(b1)
    sent = product(1,
        [own, a1[0], a1[1], b1[1], b1[0]], weight, orders[0], (aside_order, aside, right_order, right_rows)
    )
    a2, sent, left_all = tie((a2, sent, left_all))
    a3 = move(a2)
    sent = product(6, [a2[0], a2[1]], weight, orders[1], base=sent)
    b2, sent = tie((b2, sent))
    b3 = move(b2)
    got_near = exchange(sent)
    a3, sent = tie((a3, sent))
    a4 = move(a3)
    sent = product(
        6, [b2[1], b2[0], a3[0], a3[1], b3[1], b3[0]], weight, orders[2]
    )
    a4, sent = tie((a4, sent))
    sent = product(6, list(a4), weight, orders[3], base=sent)
    sent, got_near = tie((sent, got_near))
    got_far = exchange(sent)

    turned = jnp.where(tensor < tensors // 2, 1, -1)
    slots = [0, -1, 1, -2, None, None, 2, -3, 3, seqs // 2]
    slot = column(len(slots) * share)
    offset = jnp.zeros_like(slot)
    filled = jnp.ones_like(slot)
    for i, o in enumerate(slots):
        if o is None:
            filled = jnp.where(slot // share == i, 0, filled)
        else:
            offset = jnp.where(slot // share == i, o * turned, offset)
    block = (seq + offset + 2 * seqs) % seqs
    in_order = jnp.where(filled == 1, block * share + slot % share, -1)
    turn = in_order[:, None] == column(seqs * share)[None, :]
    by_line = jnp.where(filled == 1, slot % share * seqs + block, -1)
    order = (column(seqs * share)[:, None] == by_line[None, :]).astype(F32)

    cut = near * share
    both = got_near[:, cut - share : cut - share + 2].reshape(
        tensors, 2, local_blocks * share, width
    )
    both = jnp.transpose(both, (1, 0, 2, 3)).reshape(2, seqs * share, width)
    turn = turn.astype(BF16)
    resid_rows = jnp.dot(turn, both[0], preferred_element_type=F32)
    aim_rows = gain[None, :] * jnp.dot(turn, both[1], preferred_element_type=F32)
    right_proj = jnp.sum(got_near[:, cut - share + 2 :].astype(F32), axis=(0, 1))
    right_proj = right_proj.reshape(strip, rank)
    first = stats(got_near, resid_rows[:cut], aim_rows[:cut], left_all)
    target_proj = exact_dot(order, exact_dot(aim_rows, left_all, ((1,), (1,))), ((1,), (0,)))
    packed = pack(
        layers,
        share,
        got_far,
        resid_rows[cut:],
        aim_rows[cut:],
        left_all,
        first[0],
        first[1],
        target_proj,
        order,
    )
    packed = lax.all_to_all(packed, ("pipe", "seq"), 0, 0)
    totals = jnp.sum(packed.reshape(layers, seqs, packed.shape[2]), axis=1)
    cut = share * rank
    stream_proj = totals[:, :cut].reshape(strip, rank)
    target_proj = totals[:, cut : 2 * cut].reshape(strip, rank)
    square_sum = totals[:, 2 * cut : 2 * cut + share].reshape(strip, 1)
    inner = totals[:, 2 * cut + share : 2 * cut + 2 * share].reshape(strip, 1)
    root = jnp.sqrt(square_sum / D + 1e-05)
    left_proj = target_proj / root - stream_proj * (inner / (D * root * root * root))

    outer = (left_proj[:, :, None] * right_proj[:, None, :]).reshape(strip, rank * rank)
    number = jnp.arange(lengths.shape[0], dtype=jnp.int32)
    starts = jnp.sum(jnp.where(number[None, :] < number[:, None], lengths[None, :], 0), axis=1)
    ends = starts + lengths
    token = seq * block_rows + tensor * strip + jnp.arange(strip, dtype=jnp.int32)
    member = ((token[None, :] >= starts[:, None]) & (token[None, :] < ends[:, None])).astype(F32)
    partial_cores = jnp.dot(member, outer, precision=lax.Precision.HIGHEST)
    cores = jnp.sum(lax.all_to_all(partial_cores, ("seq", "tensor"), 0, 0, tiled=True), axis=0)
    scaled = cores / eigen[0]
    score, own_term = jnp.sum(query_core[0] * scaled), jnp.sum(cores * scaled)
    terms = jnp.where(lax.broadcasted_iota(jnp.int32, (layers, 2), 1) == 0, score, own_term)
    terms = jnp.sum(lax.all_to_all(terms, "pipe", 0, 0, tiled=True), axis=0)
    return (terms[0] / jnp.sqrt(terms[1] + 1e-06)).reshape(1)


def solution(mesh):
    placed = (
        P("pipe", "seq", "tensor"),
        P("pipe", "tensor", "seq"),
        P("tensor", "seq"),
        P("tensor", "seq"),
        P("seq"),
        P("pipe", "seq", None),
        P("pipe", "tensor", None),
        P("pipe", None),
        P("pipe", None),
        P(),
    )
    return jax.shard_map(
        per_device, mesh=mesh, in_specs=placed, out_specs=P(("seq", "tensor")), check_vma=False
    )
```

```python
import functools

import jax
import jax.numpy as jnp
from jax import lax
from jax.experimental import pallas as pl
from jax.experimental.pallas import tpu as pltpu
from jax.sharding import PartitionSpec as P

D = 8192
F32 = jnp.float32
BF16 = jnp.bfloat16
VMEM_BYTES = 16 << 20
PRODUCT_BYTES = 28 << 20
TILES = 4
CHUNK = 256
FLOPS_PER_MICRO = 1_150_000_000


def exact_dot(a, b, dims):
    return lax.dot_general(
        a, b, (dims, ((), ())), precision=lax.Precision.HIGHEST, preferred_element_type=F32
    )


def product_kernel(count, extras, based, *refs):
    pieces, weight, order, refs = refs[:count], refs[count], refs[count + 1], refs[count + 2 :]
    extra, refs = refs[: 2 * extras], refs[2 * extras :]
    base, refs = (refs[0], refs[1:]) if based else (None, refs)
    out, rows, tiles, sums, result, start, sems, tile_sems, out_sems, base_sem = refs
    depth = tiles.shape[1]

    def fetch(k):
        return pltpu.make_async_copy(
            weight.at[pl.ds(k * depth, depth)], tiles.at[k], tile_sems.at[k]
        )

    copies, first = [], 0
    for k, piece in enumerate(pieces):
        size = piece.shape[0]
        copies.append(pltpu.make_async_copy(piece, rows.at[pl.ds(first, size)], sems.at[k]))
        first += size
    fetch(0).start()
    for copy in copies:
        copy.start()
    for k in range(1, TILES):
        fetch(k).start()
    if based:
        first_rows = pltpu.make_async_copy(base, start, base_sem)
        first_rows.start()
    for copy in copies:
        copy.wait()
    for k in range(TILES):
        fetch(k).wait()
        value = jnp.dot(
            rows[:, k * depth : (k + 1) * depth], tiles[k], preferred_element_type=F32
        )
        if k == 0:
            sums[...] = value
        elif k < TILES - 1:
            sums[...] += value
    value = (sums[...] + value).astype(BF16)
    if based:
        first_rows.wait()
    stores = []
    for k in range(out.shape[0] // CHUNK):
        cut = pl.ds(k * CHUNK, CHUNK)
        part = jnp.dot(order[cut, :], value, preferred_element_type=F32)
        for m in range(extras):
            part += jnp.dot(
                extra[2 * m][cut, :], extra[2 * m + 1][...], preferred_element_type=F32
            )
        if based:
            part += start[cut, :].astype(F32)
        result[cut, :] = part.astype(BF16)
        stores.append(pltpu.make_async_copy(result.at[cut], out.at[cut], out_sems.at[k]))
        stores[-1].start()
    for store in stores:
        store.wait()


def product(micros, pieces, weight, order, extra=(), base=None):
    total = sum(p.shape[0] for p in pieces)
    depth, width = weight.shape
    height = order.shape[0]
    based = base is not None
    anywhere, held = pl.BlockSpec(memory_space=pltpu.HBM), pl.BlockSpec(memory_space=pltpu.VMEM)
    far = pltpu.with_memory_space_constraint
    weight = pltpu.with_memory_space_constraint(weight, pltpu.HBM)
    bases = [far(base, pltpu.HBM)] if based else []
    small = [order, *extra]
    return pl.pallas_call(
        functools.partial(product_kernel, len(pieces), len(extra) // 2, based),
        out_shape=pltpu.HBM((height, width), BF16),
        in_specs=[pl.BlockSpec(memory_space=pl.ANY)] * len(pieces) + [pl.BlockSpec(memory_space=pltpu.HBM)] + [held] * len(small) + [anywhere] * len(bases),
        out_specs=anywhere,
        scratch_shapes=[
            pltpu.VMEM((total, depth), BF16),
            pltpu.VMEM((TILES, depth // TILES, width), BF16),
            pltpu.VMEM((total, width), F32),
            pltpu.VMEM((height, width), BF16),
            pltpu.VMEM((height if based else CHUNK, width), BF16),
            pltpu.SemaphoreType.DMA((len(pieces),)),
            pltpu.SemaphoreType.DMA((TILES,)),
            pltpu.SemaphoreType.DMA((height // CHUNK,)),
            pltpu.SemaphoreType.DMA,
        ],
        compiler_params=pltpu.CompilerParams(vmem_limit_bytes=PRODUCT_BYTES),
        cost_estimate=pl.CostEstimate(
            flops=micros * FLOPS_PER_MICRO, bytes_accessed=1 << 16, transcendentals=0
        ),
    )(*pieces, weight, *small, *bases)


def reduce_rows(got, resid, aim, left, height):
    stream = resid[...] + jnp.sum(got[...].astype(F32), axis=0)
    square = jnp.sum(stream * stream, axis=1, keepdims=True)
    inner = jnp.sum(aim[...] * stream, axis=1, keepdims=True)
    lane = lax.broadcasted_iota(jnp.int32, (height, 128), 1)
    moments = jnp.where(lane == 0, square, jnp.where(lane == 1, inner, 0.0))
    return exact_dot(stream, left[...], ((1,), (1,))), moments


def stats_kernel(got, resid, aim, left, projected, moments):
    projected[...], moments[...] = reduce_rows(got, resid, aim, left, moments.shape[0])


def stats(got, resid, aim, left):
    count = got.shape[1]
    return pl.pallas_call(
        stats_kernel,
        out_shape=(
            jax.ShapeDtypeStruct((count, left.shape[0]), F32),
            jax.ShapeDtypeStruct((count, 128), F32),
        ),
        compiler_params=pltpu.CompilerParams(vmem_limit_bytes=VMEM_BYTES),
    )(got, resid, aim, left)


def pack_kernel(
    layers, share, got, resid, aim, left, first, first_moments, target, order, packed
):
    projected, moments = reduce_rows(got, resid, aim, left, got.shape[1])
    projected = jnp.concatenate([first[...], projected], axis=0)
    moments = jnp.concatenate([first_moments[...], moments], axis=0)
    projected = exact_dot(order[...], projected, ((1,), (0,)))
    moments = exact_dot(order[...], moments, ((1,), (0,)))
    blocks = order.shape[0] // share
    rank = left.shape[0] // layers
    lane = lax.broadcasted_iota(jnp.int32, (blocks, 128), 1)
    sums = jnp.zeros((blocks, 128), F32)
    for i in range(share):
        part = moments[i * blocks : (i + 1) * blocks]
        sums = jnp.where(lane == i, part[:, 0:1], sums)
        sums = jnp.where(lane == share + i, part[:, 1:2], sums)
    for l in range(layers):
        place = pl.ds(l * blocks, blocks)
        for k, source in enumerate((projected, target[...])):
            packed[place, 0, k * 128 : (k + 1) * 128] = jnp.concatenate(
                [
                    source[i * blocks : (i + 1) * blocks, l * rank : (l + 1) * rank]
                    for i in range(share)
                ],
                axis=1,
            )
        packed[place, 0, 256:384] = sums


def pack(layers, share, *operands):
    blocks = operands[-1].shape[0] // share
    return pl.pallas_call(
        functools.partial(pack_kernel, layers, share),
        out_shape=jax.ShapeDtypeStruct((layers * blocks, 1, 384), F32),
        compiler_params=pltpu.CompilerParams(vmem_limit_bytes=VMEM_BYTES),
    )(*operands)


def terms_kernel(parts, query, eigen, terms):
    cores = jnp.sum(parts[...], axis=0)
    scaled = cores / eigen[...]
    score = jnp.sum(query[...] * scaled, axis=1, keepdims=True)
    own = jnp.sum(cores * scaled, axis=1, keepdims=True)
    lane = lax.broadcasted_iota(jnp.int32, terms.shape, 1)
    terms[...] = jnp.where(lane == 0, score, own)


def per_device(
    hidden, down_weight, resid, target, gain, query_left, query_right, query_core, eigen, lengths
):
    layers = lax.axis_size("pipe")
    seqs = lax.axis_size("seq")
    tensors = lax.axis_size("tensor")
    layer = lax.axis_index("pipe")
    seq = lax.axis_index("seq")
    tensor = lax.axis_index("tensor")
    own = hidden[0]
    width = down_weight.shape[2]
    block_rows = own.shape[0]
    rank = query_left.shape[2]
    peers = tensors * layers
    share = block_rows // peers
    strip = share * layers
    local_blocks = seqs // tensors
    half = block_rows // 2
    up = [(i, (i + 1) % seqs) for i in range(seqs)]
    down = [(i, (i - 1) % seqs) for i in range(seqs)]
    tie = lax.optimization_barrier

    def move(pair):
        return lax.ppermute(pair[0], "seq", up), lax.ppermute(pair[1], "seq", down)

    def column(n):
        return jnp.arange(n, dtype=jnp.int32)

    def one_hot(source, count):
        return (source[:, None] == column(count)[None, :]).astype(BF16)

    def layout(slots):
        place = column(peers * slots * share)
        return place // (slots * share), place // share % slots, place % share

    def units(slots, first, count):
        peer, slot, line = layout(slots)
        source = (slot - first) * block_rows + peer * share + line
        inside = (slot >= first) & (slot < first + count)
        return one_hot(jnp.where(inside, source, -1), count * block_rows)

    def exchange(sent):
        return lax.all_to_all(sent.reshape(peers, -1, width), ("tensor", "pipe"), 0, 0)

    low, high = own[:half], own[half:]
    a1 = move((low, high))
    left_own = jnp.broadcast_to(
        jnp.transpose(query_left[0])[None], (layers, rank, width)
    )
    low, high, left_own = tie((low, high, left_own))
    b1 = move((high, low))
    left_all = lax.all_to_all(left_own, "pipe", 0, 0).reshape(layers * rank, width)
    weight = down_weight[0]
    aside = jnp.where(layer // (2 * local_blocks) == 0, resid, target)
    aside = lax.dynamic_slice_in_dim(aside, layer // 2 % local_blocks * block_rows, block_rows, 0)
    right_partial = jnp.dot(own, query_right[0], preferred_element_type=F32)
    right_partial = right_partial.reshape(tensors, strip * rank)
    right_high = lax.reduce_precision(right_partial, 8, 7)
    right_low = (right_partial - right_high).astype(BF16)
    right_rows = jnp.concatenate([right_high.astype(BF16), right_low], axis=0)
    right_rows = jnp.pad(right_rows, ((0, 128 - 2 * tensors), (0, 0)))

    near, far = 6, 4
    peer, slot, line = layout(near)
    spare = slot == near - 1
    aside_order = one_hot(
        jnp.where(spare & (line < 2), peer * share + layer % 2 * 2 + line, -1), block_rows
    )
    right_order = one_hot(
        jnp.where(
            spare & (line >= 2) & (peer % layers == layer),
            (line - 2) * tensors + peer // layers,
            -1,
        ),
        128,
    )
    orders = units(near, 0, 3), units(near, 3, 1), units(far, 0, 3), units(far, 3, 1)
    orders, aside_order, right_order, a1, aside = tie((orders, aside_order, right_order, a1, aside))

    a2 = move(a1)
    b1, right_rows = tie((b1, right_rows))
    b2 = move(b1)
    sent = product(1,
        [own, a1[0], a1[1], b1[1], b1[0]], weight, orders[0], (aside_order, aside, right_order, right_rows)
    )
    a2, sent, left_all = tie((a2, sent, left_all))
    a3 = move(a2)
    sent = product(6, [a2[0], a2[1]], weight, orders[1], base=sent)
    b2, sent = tie((b2, sent))
    b3 = move(b2)
    got_near = exchange(sent)
    a3, sent = tie((a3, sent))
    a4 = move(a3)
    sent = product(
        6, [b2[1], b2[0], a3[0], a3[1], b3[1], b3[0]], weight, orders[2]
    )
    a4, sent = tie((a4, sent))
    sent = product(6, list(a4), weight, orders[3], base=sent)
    sent, got_near = tie((sent, got_near))
    got_far = exchange(sent)

    turned = jnp.where(tensor < tensors // 2, 1, -1)
    slots = [0, -1, 1, -2, None, None, 2, -3, 3, seqs // 2]
    slot = column(len(slots) * share)
    offset = jnp.zeros_like(slot)
    filled = jnp.ones_like(slot)
    for i, o in enumerate(slots):
        if o is None:
            filled = jnp.where(slot // share == i, 0, filled)
        else:
            offset = jnp.where(slot // share == i, o * turned, offset)
    block = (seq + offset + 2 * seqs) % seqs
    in_order = jnp.where(filled == 1, block * share + slot % share, -1)
    turn = in_order[:, None] == column(seqs * share)[None, :]
    by_line = jnp.where(filled == 1, slot % share * seqs + block, -1)
    order = (column(seqs * share)[:, None] == by_line[None, :]).astype(F32)

    cut = near * share
    both = got_near[:, cut - share : cut - share + 2].reshape(
        tensors, 2, local_blocks * share, width
    )
    both = jnp.transpose(both, (1, 0, 2, 3)).reshape(2, seqs * share, width)
    turn = turn.astype(BF16)
    resid_rows = jnp.dot(turn, both[0], preferred_element_type=F32)
    aim_rows = gain[None, :] * jnp.dot(turn, both[1], preferred_element_type=F32)
    right_proj = jnp.sum(got_near[:, cut - share + 2 :].astype(F32), axis=(0, 1))
    right_proj = right_proj.reshape(strip, rank)
    first = stats(got_near, resid_rows[:cut], aim_rows[:cut], left_all)
    target_proj = exact_dot(order, exact_dot(aim_rows, left_all, ((1,), (1,))), ((1,), (0,)))
    packed = pack(
        layers,
        share,
        got_far,
        resid_rows[cut:],
        aim_rows[cut:],
        left_all,
        first[0],
        first[1],
        target_proj,
        order,
    )
    packed = lax.all_to_all(packed, ("pipe", "seq"), 0, 0)
    totals = jnp.sum(packed.reshape(layers, seqs, packed.shape[2]), axis=1)
    cut = share * rank
    stream_proj = totals[:, :cut].reshape(strip, rank)
    target_proj = totals[:, cut : 2 * cut].reshape(strip, rank)
    square_sum = totals[:, 2 * cut : 2 * cut + share].reshape(strip, 1)
    inner = totals[:, 2 * cut + share : 2 * cut + 2 * share].reshape(strip, 1)
    root = jnp.sqrt(square_sum / D + 1e-05)
    left_proj = target_proj / root - stream_proj * (inner / (D * root * root * root))

    outer = (left_proj[:, :, None] * right_proj[:, None, :]).reshape(strip, rank * rank)
    number = jnp.arange(lengths.shape[0], dtype=jnp.int32)
    starts = jnp.sum(jnp.where(number[None, :] < number[:, None], lengths[None, :], 0), axis=1)
    ends = starts + lengths
    token = seq * block_rows + tensor * strip + jnp.arange(strip, dtype=jnp.int32)
    member = ((token[None, :] >= starts[:, None]) & (token[None, :] < ends[:, None])).astype(F32)
    partial_cores = jnp.dot(member, outer, precision=lax.Precision.HIGHEST)
    parts = lax.all_to_all(partial_cores, ("seq", "tensor"), 0, 0, tiled=True)
    terms = pl.pallas_call(
        terms_kernel,
        out_shape=jax.ShapeDtypeStruct((layers, 2), F32),
        compiler_params=pltpu.CompilerParams(vmem_limit_bytes=VMEM_BYTES),
    )(parts.reshape(parts.shape[0], 1, rank * rank), query_core, eigen)
    terms = jnp.sum(lax.all_to_all(terms, "pipe", 0, 0, tiled=True), axis=0)
    return (terms[0] / jnp.sqrt(terms[1] + 1e-06)).reshape(1)


def solution(mesh):
    placed = (
        P("pipe", "seq", "tensor"),
        P("pipe", "tensor", "seq"),
        P("tensor", "seq"),
        P("tensor", "seq"),
        P("seq"),
        P("pipe", "seq", None),
        P("pipe", "tensor", None),
        P("pipe", None),
        P("pipe", None),
        P(),
    )
    return jax.shard_map(
        per_device, mesh=mesh, in_specs=placed, out_specs=P(("seq", "tensor")), check_vma=False
    )
```
